32 devices in a mesh: row: 4 (over x, core), col: 8 (over z, y).
Axes of the slice: x: 2, y: 2, z: 4, core: 2. Of those that a mesh axis runs over, the one named last changes fastest.
Arguments:
- p_valence: bfloat16 [4096, 4096], P('row', 'col'), as said below
- p_conduction: bfloat16 [4096, 4096], P('row', 'col'), as said below
- trial_vectors: bfloat16 [2, 4096, 4096], P(None, 'row', 'col'), may hold values from -6 to 6
- mask_valence: int32 [32, 32], replicated, may hold values from 0 to 1, as said below
- mask_conduction: int32 [32, 32], replicated, may hold values from 0 to 1, as said below
- mask_trial: int32 [32, 32], replicated, may hold values 0 or 1
- orbitals: bfloat16 [32, 128, 8192], P('row'), may hold values from -0.29882812 to 0.29882812
- sphere_starts: int32 [32], replicated, may hold values from 0 to 16, as said below
Outputs:
- kernel: bfloat16 [2, 4096, 4096], P(None, 'row', 'col')
- density: float32 [2, 16384], P(None, ('row', 'col'))
The draws below stay inside these ranges and needn't reach their ends.
Inputs may be any that keep to these rules, and one draw needn't show every extreme that they name: `mask_valence`: symmetric, ones on the block diagonal and next to it. `mask_conduction`: symmetric, ones on the block diagonal and next to it. `p_valence`: symmetric. `p_conduction`: symmetric. `sphere_starts`: the first block's start is 0 and the last block's 32 - 16.
All inputs are finite; a program needn't handle non-finite values.
Results may differ from the reference program's by a relative error of at most 0.0049.
Values may be sent and summed in bfloat16 or wider, within the bound.
A program may use at most 320 MiB of HBM per device.

```python
import math
import jax
import jax.numpy as jnp
from jax import lax

BS = 128
NB = 32
SPAN = 16
SP = 512
NVEC = 2
NO = 4096
NSLAB = 32
N_ROW = 4
N_COL = 8


def symmetric_values(key):
    scale = 1.0 / math.sqrt(BS * (3.0 + (NB - 3) / 4.0))
    base = jax.random.normal(key, (NB * BS, NB * BS), jnp.float32)
    return ((base + base.T) * (scale * 0.70710678)).astype(jnp.bfloat16)


def symmetric_mask(key):
    coins = jax.random.randint(key, (NB, NB), 0, 4)
    chosen = coins == 0
    indices = jnp.arange(NB)
    banded = jnp.abs(indices[:, None] - indices[None, :]) <= 1
    return (chosen | chosen.T | banded).astype(jnp.int32)


def draw_p_valence(key, part):
    return symmetric_values(jax.random.fold_in(key, 11))


def draw_p_conduction(key, part):
    return symmetric_values(jax.random.fold_in(key, 12))


def draw_mask_valence(key, part):
    return symmetric_mask(jax.random.fold_in(key, 21))


def draw_mask_conduction(key, part):
    return symmetric_mask(jax.random.fold_in(key, 22))


def draw_sphere_starts(key, part):
    last_start = NSLAB - SPAN
    per_row = NB // N_ROW
    half_rows = max(N_ROW // 2, 1)
    stride = max(NSLAB // 2 // per_row, 1)
    indices = jnp.arange(NB, dtype=jnp.int32)
    placed = indices // per_row % half_rows * N_COL + indices % per_row * stride
    jitter = jax.random.randint(jax.random.fold_in(key, 31), (NB,), -2, 3)
    placed = jnp.clip(placed + jitter, 0, last_start)
    placed = placed.at[0].set(0).at[NB - 1].set(last_start)
    return placed.astype(jnp.int32)


def place_ends(entries, own_key, smallest, top_value):
    extent = entries.shape
    index_at = [jax.random.randint(jax.random.fold_in(own_key, axis), (), 0, extent[axis]) for axis in range(len(extent))]
    entries = entries.at[tuple(index_at)].set(smallest)
    longest = extent.index(max(extent))
    index_at[longest] = (index_at[longest] + 1) % extent[longest]
    return entries.at[tuple(index_at)].set(top_value)


def block_scale(key, extent, split, smallest, top_value):
    def one(position, blocks):
        draws = jax.random.uniform(jax.random.fold_in(jax.random.fold_in(key, 6), position), (blocks,), jnp.float32, smallest / len(split), top_value / len(split))
        return jnp.repeat(jnp.exp(draws), extent[position] // blocks).reshape((-1,) + (1,) * (len(extent) - position - 1))

    level = one(*split[0])
    for cut in split[1:]:
        level = level * one(*cut)
    return level


def scatter_about(own_key, dims, scale, bound, pieces=(), held_as=jnp.bfloat16):
    result = scale * jax.random.normal(own_key, dims, jnp.float32)
    if pieces:
        result = result * block_scale(own_key, dims, pieces, -0.22, 0.18)
    return jnp.clip(result, -bound, bound).astype(held_as)


def setup_inputs(seed: int = 0) -> dict:
    keys = jax.random.split(jax.random.key(seed), 9)
    return {
        "p_valence": draw_p_valence(jax.random.fold_in(keys[8], 71), 0),
        "p_conduction": draw_p_conduction(jax.random.fold_in(keys[8], 71), 0),
        "trial_vectors": scatter_about(keys[2], (NVEC, NO, NO), 1.0, 6.0, ((1, 4), (2, 8))),
        "mask_valence": draw_mask_valence(jax.random.fold_in(keys[8], 71), 0),
        "mask_conduction": draw_mask_conduction(jax.random.fold_in(keys[8], 71), 0),
        "mask_trial": place_ends((jax.random.randint(keys[5], (NB, NB), 0, 3) < 1).astype(jnp.int32), jax.random.fold_in(keys[5], 1), 0, 1),
        "orbitals": scatter_about(keys[6], (NB, BS, SPAN * SP), 0.05, 0.29882812, ((0, 4),)),
        "sphere_starts": draw_sphere_starts(jax.random.fold_in(keys[8], 71), 0),
    }


def expand(block_mask):
    widened = jnp.repeat(block_mask, BS, axis=0)
    return jnp.repeat(widened, BS, axis=1).astype(jnp.bfloat16)


def reference(p_valence, p_conduction, trial_vectors, mask_valence, mask_conduction, mask_trial, orbitals, sphere_starts):
    valence = p_valence * expand(mask_valence)
    conduction = p_conduction * expand(mask_conduction)
    trial_mask = expand(mask_trial)
    trials = trial_vectors * trial_mask[None]
    response = jnp.einsum("vik,kj->vij", trials.astype(jnp.float32), conduction.astype(jnp.float32)).astype(jnp.bfloat16)
    kernel_sum = jnp.einsum("ik,vkj->vij", valence.astype(jnp.float32), response.astype(jnp.float32))
    kernel = (kernel_sum * trial_mask.astype(jnp.float32)[None]).astype(jnp.bfloat16)
    shaped = orbitals.reshape(NB, BS, SPAN, SP)
    padded = jnp.pad(shaped, ((0, 0), (0, 0), (SPAN, SPAN), (0, 0)))

    def take_frame(orbital_block, offset):
        return lax.dynamic_slice_in_dim(orbital_block, offset, SPAN, 1)

    def add_block(index, density_grid):
        index = index.astype(jnp.int32)
        own_start = lax.dynamic_slice_in_dim(sphere_starts, index, 1, 0)[0]
        offsets = jnp.clip(own_start - sphere_starts + SPAN, 0, 2 * SPAN).astype(jnp.int32)
        frames = jax.vmap(take_frame)(padded, offsets).reshape(NB, BS, SPAN * SP)
        kernel_rows = lax.dynamic_slice_in_dim(kernel, index * BS, BS, 1).reshape(NVEC, BS, NB, BS)
        applied = jnp.einsum("vmjn,jnp->vmp", kernel_rows.astype(jnp.float32), frames.astype(jnp.float32))
        own_values = lax.dynamic_slice_in_dim(orbitals, index, 1, 0)[0].astype(jnp.float32)
        contrib = jnp.sum(own_values[None] * applied, axis=1).reshape(NVEC, SPAN, SP)
        zero_index = jnp.zeros((), jnp.int32)
        current = lax.dynamic_slice(density_grid, (zero_index, own_start, zero_index), (NVEC, SPAN, SP))
        return lax.dynamic_update_slice(density_grid, current + contrib, (zero_index, own_start, zero_index))

    density_grid = lax.fori_loop(0, NB, add_block, jnp.zeros((NVEC, NSLAB, SP), jnp.float32))
    return kernel, density_grid.reshape(NVEC, NSLAB * SP)
```

```python
import functools

import jax
import jax.numpy as jnp
from jax import lax
from jax.experimental import pallas as pl
from jax.experimental.pallas import tpu as pltpu
from jax.sharding import PartitionSpec as P

BS = 128
SPAN = 16
SP = 512


def broadcast(x, axis, root):
    mine = lax.axis_index(axis) == root
    return lax.psum(jnp.where(mine, x, jnp.zeros_like(x)), axis)


def masked(values, block_mask, row_index, col_index):
    leading_dims = values.shape[:-2]
    row_blocks = values.shape[-2] // BS
    col_blocks = values.shape[-1] // BS
    tile_mask = lax.dynamic_slice(
        block_mask, (row_index * row_blocks, col_index * col_blocks), (row_blocks, col_blocks)
    ).astype(values.dtype)
    shaped = values.reshape(leading_dims + (row_blocks, BS, col_blocks, BS))
    return (shaped * tile_mask[:, None, :, None]).reshape(values.shape)


def collocate_kernel(row_blocks, col_blocks, starts_rows, starts_cols, kernel_ref, *refs):
    row_refs = refs[:row_blocks]
    col_refs = refs[row_blocks : row_blocks + col_blocks]
    out_ref, frame_ref = refs[row_blocks + col_blocks :]
    slab = pl.program_id(0)
    for j in range(col_blocks):
        shift = slab - starts_cols[j]
        active = (shift >= 0) & (shift < SPAN)

        @pl.when(active)
        def _():
            frame_ref[j * BS : (j + 1) * BS, :] = col_refs[j][0]

        @pl.when(jnp.logical_not(active))
        def _():
            frame_ref[j * BS : (j + 1) * BS, :] = jnp.zeros((BS, SP), frame_ref.dtype)

    out_ref[...] = jnp.zeros_like(out_ref)
    for i in range(row_blocks):
        shift = slab - starts_rows[i]

        @pl.when((shift >= 0) & (shift < SPAN))
        def _():
            own = row_refs[i][0].astype(jnp.float32)
            for v in range(kernel_ref.shape[0]):
                applied = jnp.dot(
                    kernel_ref[v, i * BS : (i + 1) * BS, :],
                    frame_ref[...],
                    preferred_element_type=jnp.float32,
                )
                out_ref[0, v : v + 1, :] += jnp.sum(own * applied, axis=0, keepdims=True)


def orbital_spec(block, which):
    def index_map(slab, starts_rows, starts_cols):
        start = (starts_rows, starts_cols)[which][block]
        return block, 0, jnp.clip(slab - start, 0, SPAN - 1)

    return pl.BlockSpec((1, BS, SP), index_map)


def collocate(kernel, orbitals, partner, starts_rows, starts_cols, slab_count):
    vector_count = kernel.shape[0]
    row_blocks = orbitals.shape[0]
    col_blocks = partner.shape[0]
    return pl.pallas_call(
        functools.partial(collocate_kernel, row_blocks, col_blocks),
        out_shape=jax.ShapeDtypeStruct((slab_count, vector_count, SP), jnp.float32),
        grid_spec=pltpu.PrefetchScalarGridSpec(
            num_scalar_prefetch=2,
            grid=(slab_count,),
            in_specs=[pl.BlockSpec(kernel.shape, lambda slab, a, b: (0, 0, 0))]
            + [orbital_spec(i, 0) for i in range(row_blocks)]
            + [orbital_spec(j, 1) for j in range(col_blocks)],
            out_specs=pl.BlockSpec((1, vector_count, SP), lambda slab, a, b: (slab, 0, 0)),
            scratch_shapes=[pltpu.VMEM((col_blocks * BS, SP), jnp.bfloat16)],
        ),
        compiler_params=pltpu.CompilerParams(dimension_semantics=("arbitrary",)),
    )(starts_rows, starts_cols, kernel, *([orbitals] * row_blocks), *([partner] * col_blocks))


def local(
    p_valence,
    p_conduction,
    trial_vectors,
    mask_valence,
    mask_conduction,
    mask_trial,
    orbitals,
    sphere_starts,
):
    row_index = lax.axis_index("row")
    col_index = lax.axis_index("col")
    valence = masked(p_valence, mask_valence, row_index, col_index)
    conduction = masked(p_conduction, mask_conduction, row_index, col_index)
    trials = masked(trial_vectors, mask_trial, row_index, col_index)
    vector_count = trials.shape[0]
    local_rows = trials.shape[1]
    local_cols = trials.shape[2]
    panels = lax.all_gather(trials, "col", axis=2, tiled=True)
    response = jnp.einsum(
        "vik,kj->vij",
        panels,
        lax.all_gather(conduction, "row", axis=0, tiled=True),
        preferred_element_type=jnp.float32,
    )
    response_half = response.astype(jnp.bfloat16)
    gathered = lax.all_gather(response_half, "row", axis=1, tiled=True)
    kernel_sum = jnp.einsum(
        "ik,vkj->vij",
        lax.all_gather(valence, "col", axis=1, tiled=True),
        gathered,
        preferred_element_type=jnp.float32,
    )
    kernel = masked(kernel_sum, mask_trial, row_index, col_index).astype(jnp.bfloat16)
    row_blocks = local_rows // BS
    col_blocks = local_cols // BS
    ratio = lax.axis_size("col") // lax.axis_size("row")
    own_part = lax.dynamic_slice_in_dim(orbitals, col_index % ratio * col_blocks, col_blocks, 0)
    partner = broadcast(own_part, "row", col_index // ratio)
    starts_rows = lax.dynamic_slice_in_dim(sphere_starts, row_index * row_blocks, row_blocks, 0)
    starts_cols = lax.dynamic_slice_in_dim(sphere_starts, col_index * col_blocks, col_blocks, 0)
    slab_count = lax.axis_size("row") * lax.axis_size("col")
    density_grid = collocate(kernel, orbitals, partner, starts_rows, starts_cols, slab_count)
    own_slab = lax.psum_scatter(density_grid, ("row", "col"), scatter_dimension=0, tiled=True)
    density = own_slab.reshape(vector_count, SP)
    return (kernel, density)


def solution(mesh):
    placed = (
        P("row", "col"),
        P("row", "col"),
        P(None, "row", "col"),
        P(),
        P(),
        P(),
        P("row", None, None),
        P(),
    )
    return jax.shard_map(
        local,
        mesh=mesh,
        in_specs=placed,
        out_specs=(P(None, "row", "col"), P(None, ("row", "col"))),
        check_vma=False,
    )
```

```python
import functools

import jax
import jax.numpy as jnp
from jax import lax
from jax.experimental import pallas as pl
from jax.experimental.pallas import tpu as pltpu
from jax.sharding import PartitionSpec as P

BS = 128
SPAN = 16
SP = 512


def masked(values, block_mask, row_index, col_index):
    leading_dims = values.shape[:-2]
    row_blocks = values.shape[-2] // BS
    col_blocks = values.shape[-1] // BS
    tile_mask = lax.dynamic_slice(
        block_mask, (row_index * row_blocks, col_index * col_blocks), (row_blocks, col_blocks)
    ).astype(values.dtype)
    shaped = values.reshape(leading_dims + (row_blocks, BS, col_blocks, BS))
    return (shaped * tile_mask[:, None, :, None]).reshape(values.shape)


def collocate_kernel(row_blocks, col_blocks, starts_rows, starts_cols, kernel_ref, *refs):
    row_refs = refs[:row_blocks]
    col_refs = refs[row_blocks : row_blocks + col_blocks]
    out_ref, frame_ref = refs[row_blocks + col_blocks :]
    slab = pl.program_id(0)
    for j in range(col_blocks):
        shift = slab - starts_cols[j]
        active = (shift >= 0) & (shift < SPAN)

        @pl.when(active)
        def _():
            frame_ref[j * BS : (j + 1) * BS, :] = col_refs[j][0]

        @pl.when(jnp.logical_not(active))
        def _():
            frame_ref[j * BS : (j + 1) * BS, :] = jnp.zeros((BS, SP), frame_ref.dtype)

    out_ref[...] = jnp.zeros_like(out_ref)
    for i in range(row_blocks):
        shift = slab - starts_rows[i]

        @pl.when((shift >= 0) & (shift < SPAN))
        def _():
            own = row_refs[i][0].astype(jnp.float32)
            for v in range(kernel_ref.shape[0]):
                applied = jnp.dot(
                    kernel_ref[v, i * BS : (i + 1) * BS, :],
                    frame_ref[...],
                    preferred_element_type=jnp.float32,
                )
                out_ref[0, v : v + 1, :] += jnp.sum(own * applied, axis=0, keepdims=True)


def orbital_spec(block, which):
    def index_map(slab, starts_rows, starts_cols):
        start = (starts_rows, starts_cols)[which][block]
        return block, 0, jnp.clip(slab - start, 0, SPAN - 1)

    return pl.BlockSpec((1, BS, SP), index_map)


def collocate(kernel, orbitals, partner, starts_rows, starts_cols, slab_count):
    vector_count = kernel.shape[0]
    row_blocks = orbitals.shape[0]
    col_blocks = partner.shape[0]
    return pl.pallas_call(
        functools.partial(collocate_kernel, row_blocks, col_blocks),
        out_shape=jax.ShapeDtypeStruct((slab_count, vector_count, SP), jnp.float32),
        grid_spec=pltpu.PrefetchScalarGridSpec(
            num_scalar_prefetch=2,
            grid=(slab_count,),
            in_specs=[pl.BlockSpec(kernel.shape, lambda slab, a, b: (0, 0, 0))]
            + [orbital_spec(i, 0) for i in range(row_blocks)]
            + [orbital_spec(j, 1) for j in range(col_blocks)],
            out_specs=pl.BlockSpec((1, vector_count, SP), lambda slab, a, b: (slab, 0, 0)),
            scratch_shapes=[pltpu.VMEM((col_blocks * BS, SP), jnp.bfloat16)],
        ),
        compiler_params=pltpu.CompilerParams(dimension_semantics=("arbitrary",)),
    )(starts_rows, starts_cols, kernel, *([orbitals] * row_blocks), *([partner] * col_blocks))


def ring_place(col, size):
    odd = col % 2
    return (col // 2) * (1 - odd) + (size - 1 - col // 2) * odd


def ring_col(place, size):
    far = place // (size // 2)
    return 2 * place * (1 - far) + (2 * (size - 1 - place) + 1) * far


def remote(src, dst, send_sem, recv_sem, **where):
    return pltpu.make_async_remote_copy(
        src_ref=src,
        dst_ref=dst,
        send_sem=send_sem,
        recv_sem=recv_sem,
        device_id=where,
        device_id_type=pl.DeviceIdType.MESH,
    )


def ring_copy(mine, panel, place, size, step, way, send, recv):
    rows, width = mine.shape[1] // 2, mine.shape[2]
    sign = 1 - 2 * way
    owner = ring_col((place - sign * step + size) % size, size)
    half = pl.ds(way * rows, rows)
    held = panel.at[:, half, pl.ds(pl.multiple_of(owner * width, width), width)]
    src = mine.at[:, half, :] if step == 0 else held
    target = ring_col((place + sign + size) % size, size)
    return remote(src, held, send.at[way, step], recv.at[way, step], col=target)


def row_part(stack, row, rows):
    return stack.at[:, pl.ds(pl.multiple_of(row * rows, rows), rows), :]


def gather_kernel(n_row, n_col, with_orbitals, *refs):
    refs = list(refs)
    ring_in, row_in = refs[:2]
    del refs[:2]
    orbitals = refs.pop(0) if with_orbitals else None
    panel, stack = refs[:2]
    del refs[:2]
    partner = refs.pop(0) if with_orbitals else None
    ring_hold, row_hold = refs[:2]
    del refs[:2]
    orbital_hold = refs.pop(0) if with_orbitals else None
    hold_in, hold_out, ring_send, ring_recv, row_send, row_recv = refs[:6]
    orbital_send, orbital_recv = refs[6:] if with_orbitals else (None, None)

    row, col = lax.axis_index("row"), lax.axis_index("col")
    place = ring_place(col, n_col)
    chips = n_row // 2
    chip, core = row // 2, row % 2
    pair = row + 1 - 2 * core
    rows, width = row_in.shape[1], ring_in.shape[2]

    barrier = pltpu.get_barrier_semaphore()
    for sign in (1, -1):
        pl.semaphore_signal(
            barrier,
            inc=1,
            device_id={"col": ring_col((place + sign + n_col) % n_col, n_col)},
            device_id_type=pl.DeviceIdType.MESH,
        )
    for d in range(1, n_row):
        pl.semaphore_signal(
            barrier,
            inc=1,
            device_id={"row": (row + d) % n_row},
            device_id_type=pl.DeviceIdType.MESH,
        )
    pl.semaphore_wait(barrier, n_row + 1)

    def ring(step, way):
        return ring_copy(ring_in, panel, place, n_col, step, way, ring_send, ring_recv)

    def across(d):
        target = pair if d == 0 else (chip + d) % chips * 2 + core
        return remote(
            row_in, row_part(stack, row, rows), row_send.at[d], row_recv.at[d], row=target
        )

    def onward(d):
        held = row_part(stack, (chip - d + chips) % chips * 2 + core, rows)
        k = chips - 1 + d
        return remote(held, held, row_send.at[k], row_recv.at[k], row=pair)

    ring(0, 0).start()
    ring(0, 1).start()
    for d in range(1, chips):
        across(d).start()
    across(0).start()

    if with_orbitals:
        blocks = partner.shape[0]
        part = blocks // 2
        ratio = n_col // n_row
        source = col // ratio
        own = orbitals.at[pl.ds(col % ratio * blocks, blocks)]
        here = chip == source // 2
        is_source = row == source

        def to_pair():
            return remote(own, partner, orbital_send.at[0], orbital_recv.at[0], row=pair)

        def to_chip(d, h):
            k = 1 + 2 * (d - 1) + h
            return remote(
                orbitals.at[pl.ds(col % ratio * blocks + h * part, part)],
                partner.at[pl.ds(h * part, part)],
                orbital_send.at[k],
                orbital_recv.at[1],
                row=(chip + d) % chips * 2 + h,
            )

        def half_onward():
            held = partner.at[pl.ds(core * part, part)]
            return remote(
                held, held, orbital_send.at[2 * chips - 1], orbital_recv.at[2], row=pair
            )

        @pl.when(is_source)
        def _():
            for d in range(1, chips):
                for h in range(2):
                    to_chip(d, h).start()
            to_pair().start()

    ins = [(ring_in, ring_hold), (row_in, row_hold)]
    outs = [
        (ring_hold, panel.at[:, :, pl.ds(pl.multiple_of(col * width, width), width)]),
        (row_hold, row_part(stack, row, rows)),
    ]
    for k in range(2):
        pltpu.make_async_copy(*ins[k], hold_in.at[k]).start()
    for k in range(2):
        pltpu.make_async_copy(*ins[k], hold_in.at[k]).wait()
        pltpu.make_async_copy(*outs[k], hold_out.at[k]).start()
    if with_orbitals:

        @pl.when(is_source)
        def _():
            fetch = pltpu.make_async_copy(own, orbital_hold, hold_in.at[2])
            fetch.start()
            fetch.wait()
            pltpu.make_async_copy(orbital_hold, partner, hold_out.at[2]).start()

    for step in range(n_col - 1):
        for way in range(2):
            ring(step, way).wait_recv()
            if step < n_col - 2:
                ring(step + 1, way).start()
        if step == min(2, n_col - 2):
            for d in range(1, chips):
                across(d).wait_recv()
                onward(d).start()
        if with_orbitals and step == n_col - 3:

            @pl.when(jnp.logical_not(here))
            def _():
                to_chip(1, 0).wait_recv()
                half_onward().start()

    across(0).wait_recv()
    for d in range(1, chips):
        onward(d).wait_recv()
        onward(d).wait_send()
        across(d).wait_send()
    across(0).wait_send()
    if with_orbitals:

        @pl.when(is_source)
        def _():
            for d in range(1, chips):
                for h in range(2):
                    to_chip(d, h).wait_send()
            to_pair().wait_send()
            pltpu.make_async_copy(orbital_hold, partner, hold_out.at[2]).wait()

        @pl.when(here & jnp.logical_not(is_source))
        def _():
            to_pair().wait_recv()

        @pl.when(jnp.logical_not(here))
        def _():
            half_onward().wait_recv()
            half_onward().wait_send()

    for step in range(n_col - 1):
        for way in range(2):
            ring(step, way).wait_send()
    for k in range(2):
        pltpu.make_async_copy(*outs[k], hold_out.at[k]).wait()


def gather(ring_in, row_in, orbitals, collective_id):
    n_row, n_col = lax.axis_size("row"), lax.axis_size("col")
    lead, rows, width = ring_in.shape
    panel = jax.ShapeDtypeStruct((lead, rows, n_col * width), ring_in.dtype)
    stack = jax.ShapeDtypeStruct(
        (row_in.shape[0], n_row * row_in.shape[1], row_in.shape[2]), row_in.dtype
    )
    operands, results = [ring_in, row_in], [panel, stack]
    holds = [pltpu.VMEM(ring_in.shape, ring_in.dtype), pltpu.VMEM(row_in.shape, row_in.dtype)]
    dma = pltpu.SemaphoreType.DMA
    sems = [dma((3,)), dma((3,)), dma((2, n_col - 1)), dma((2, n_col - 1))]
    sems += [dma((n_row - 1,)), dma((n_row - 1,))]
    if orbitals is not None:
        blocks = orbitals.shape[0] * n_row // n_col
        partner = (blocks,) + orbitals.shape[1:]
        operands.append(orbitals)
        results.append(jax.ShapeDtypeStruct(partner, orbitals.dtype))
        holds.append(pltpu.VMEM(partner, orbitals.dtype))
        sems += [dma((n_row,)), dma((3,))]
    return pl.pallas_call(
        functools.partial(gather_kernel, n_row, n_col, orbitals is not None),
        out_shape=results,
        in_specs=[pl.BlockSpec(memory_space=pl.ANY)] * len(operands),
        out_specs=[pl.BlockSpec(memory_space=pl.ANY)] * len(results),
        scratch_shapes=holds + sems,
        compiler_params=pltpu.CompilerParams(
            collective_id=collective_id, has_side_effects=True
        ),
    )(*operands)


def reduce_kernel(axis, size, in_ref, out_ref, landed, own_sem, send, recv):
    me = lax.axis_index(axis)
    barrier = pltpu.get_barrier_semaphore()
    for d in range(1, size):
        pl.semaphore_signal(
            barrier,
            inc=1,
            device_id={axis: (me + d) % size},
            device_id_type=pl.DeviceIdType.MESH,
        )
    own = pltpu.make_async_copy(in_ref.at[me], landed.at[0], own_sem)
    own.start()
    pl.semaphore_wait(barrier, size - 1)
    copies = []
    for d in range(1, size):
        target = (me + d) % size
        copies.append(
            remote(in_ref.at[target], landed.at[d], send.at[d], recv.at[d], **{axis: target})
        )
        copies[-1].start()
    own.wait()
    for copy in copies:
        copy.wait_recv()
    out_ref[...] = jnp.sum(landed[...], axis=0)
    for copy in copies:
        copy.wait_send()


def reduce_over(axis, terms, collective_id):
    size = terms.shape[0]
    dma = pltpu.SemaphoreType.DMA
    return pl.pallas_call(
        functools.partial(reduce_kernel, axis, size),
        out_shape=jax.ShapeDtypeStruct(terms.shape[1:], terms.dtype),
        in_specs=[pl.BlockSpec(memory_space=pl.ANY)],
        out_specs=pl.BlockSpec(memory_space=pltpu.VMEM),
        scratch_shapes=[pltpu.VMEM(terms.shape, terms.dtype), dma, dma((size,)), dma((size,))],
        compiler_params=pltpu.CompilerParams(
            collective_id=collective_id, has_side_effects=True
        ),
    )(terms)


def local(
    p_valence,
    p_conduction,
    trial_vectors,
    mask_valence,
    mask_conduction,
    mask_trial,
    orbitals,
    sphere_starts,
):
    row_index = lax.axis_index("row")
    col_index = lax.axis_index("col")
    valence = masked(p_valence, mask_valence, row_index, col_index)
    conduction = masked(p_conduction, mask_conduction, row_index, col_index)
    trials = masked(trial_vectors, mask_trial, row_index, col_index)
    vector_count = trials.shape[0]
    local_rows = trials.shape[1]
    local_cols = trials.shape[2]
    panels, conduction_cols, partner = gather(trials, conduction[None], orbitals, 0)
    response = jnp.einsum(
        "vik,kj->vij", panels, conduction_cols[0], preferred_element_type=jnp.float32
    ).astype(jnp.bfloat16)
    valence_rows, gathered = gather(valence[None], response, None, 1)
    kernel_sum = jnp.einsum(
        "ik,vkj->vij", valence_rows[0], gathered, preferred_element_type=jnp.float32
    )
    kernel = masked(kernel_sum, mask_trial, row_index, col_index).astype(jnp.bfloat16)
    row_blocks = local_rows // BS
    col_blocks = local_cols // BS
    starts_rows = lax.dynamic_slice_in_dim(sphere_starts, row_index * row_blocks, row_blocks, 0)
    starts_cols = lax.dynamic_slice_in_dim(sphere_starts, col_index * col_blocks, col_blocks, 0)
    slab_count = lax.axis_size("row") * lax.axis_size("col")
    density_grid = collocate(kernel, orbitals, partner, starts_rows, starts_cols, slab_count)
    n_row, n_col = lax.axis_size("row"), lax.axis_size("col")
    terms = density_grid.reshape(n_row, n_col, vector_count, SP)
    density = reduce_over("col", reduce_over("row", terms, 2), 3)
    return (kernel, density)


def solution(mesh):
    placed = (
        P("row", "col"),
        P("row", "col"),
        P(None, "row", "col"),
        P(),
        P(),
        P(),
        P("row", None, None),
        P(),
    )
    return jax.shard_map(
        local,
        mesh=mesh,
        in_specs=placed,
        out_specs=(P(None, "row", "col"), P(None, ("row", "col"))),
        check_vma=False,
    )
```

```python
import functools

import jax
import jax.numpy as jnp
from jax import lax
from jax.experimental import pallas as pl
from jax.experimental.pallas import tpu as pltpu
from jax.sharding import PartitionSpec as P

BS = 128
SPAN = 16
SP = 512


def masked(values, block_mask, row_index, col_index):
    leading_dims = values.shape[:-2]
    row_blocks = values.shape[-2] // BS
    col_blocks = values.shape[-1] // BS
    tile_mask = lax.dynamic_slice(
        block_mask, (row_index * row_blocks, col_index * col_blocks), (row_blocks, col_blocks)
    ).astype(values.dtype)
    shaped = values.reshape(leading_dims + (row_blocks, BS, col_blocks, BS))
    return (shaped * tile_mask[:, None, :, None]).reshape(values.shape)


def collocate_kernel(row_blocks, col_blocks, starts_rows, starts_cols, kernel_ref, *refs):
    row_refs = refs[:row_blocks]
    col_refs = refs[row_blocks : row_blocks + col_blocks]
    out_ref, frame_ref = refs[row_blocks + col_blocks :]
    slab = pl.program_id(0)
    for j in range(col_blocks):
        shift = slab - starts_cols[j]
        active = (shift >= 0) & (shift < SPAN)

        @pl.when(active)
        def _():
            frame_ref[j * BS : (j + 1) * BS, :] = col_refs[j][0]

        @pl.when(jnp.logical_not(active))
        def _():
            frame_ref[j * BS : (j + 1) * BS, :] = jnp.zeros((BS, SP), frame_ref.dtype)

    out_ref[...] = jnp.zeros_like(out_ref)
    for i in range(row_blocks):
        shift = slab - starts_rows[i]

        @pl.when((shift >= 0) & (shift < SPAN))
        def _():
            own = row_refs[i][0].astype(jnp.float32)
            vectors = kernel_ref.shape[0]
            left = kernel_ref[:, i * BS : (i + 1) * BS, :].reshape(vectors * BS, col_blocks * BS)
            applied = jnp.dot(left, frame_ref[...], preferred_element_type=jnp.float32)
            for v in range(vectors):
                term = own * applied[v * BS : (v + 1) * BS]
                out_ref[0, v : v + 1, :] += jnp.sum(term, axis=0, keepdims=True)


def orbital_spec(block, which):
    def index_map(slab, starts_rows, starts_cols):
        start = (starts_rows, starts_cols)[which][block]
        return block, 0, jnp.clip(slab - start, 0, SPAN - 1)

    return pl.BlockSpec((1, BS, SP), index_map)


def collocate(kernel, orbitals, partner, starts_rows, starts_cols, slab_count):
    vector_count = kernel.shape[0]
    row_blocks = orbitals.shape[0]
    col_blocks = partner.shape[0]
    return pl.pallas_call(
        functools.partial(collocate_kernel, row_blocks, col_blocks),
        out_shape=jax.ShapeDtypeStruct((slab_count, vector_count, SP), jnp.float32),
        grid_spec=pltpu.PrefetchScalarGridSpec(
            num_scalar_prefetch=2,
            grid=(slab_count,),
            in_specs=[pl.BlockSpec(kernel.shape, lambda slab, a, b: (0, 0, 0))]
            + [orbital_spec(i, 0) for i in range(row_blocks)]
            + [orbital_spec(j, 1) for j in range(col_blocks)],
            out_specs=pl.BlockSpec((1, vector_count, SP), lambda slab, a, b: (slab, 0, 0)),
            scratch_shapes=[pltpu.VMEM((col_blocks * BS, SP), jnp.bfloat16)],
        ),
        compiler_params=pltpu.CompilerParams(dimension_semantics=("arbitrary",)),
    )(starts_rows, starts_cols, kernel, *([orbitals] * row_blocks), *([partner] * col_blocks))


def ring_place(col, size):
    odd = col % 2
    return (col // 2) * (1 - odd) + (size - 1 - col // 2) * odd


def ring_col(place, size):
    far = place // (size // 2)
    return 2 * place * (1 - far) + (2 * (size - 1 - place) + 1) * far


def remote(src, dst, send_sem, recv_sem, **where):
    return pltpu.make_async_remote_copy(
        src_ref=src,
        dst_ref=dst,
        send_sem=send_sem,
        recv_sem=recv_sem,
        device_id=where,
        device_id_type=pl.DeviceIdType.MESH,
    )


def ring_copy(mine, panel, used, place, size, step, way, send, recv):
    rows = used // 2
    sign = 1 - 2 * way
    owner = ring_col((place - sign * step + size) % size, size)
    half = pl.ds(way * rows, rows)
    held = panel.at[owner, :, half, :]
    src = mine.at[:, half, :] if step == 0 else held
    target = ring_col((place + sign + size) % size, size)
    return remote(src, held, send.at[way, step], recv.at[way, step], col=target)


def row_part(stack, row, rows):
    return stack.at[:, pl.ds(pl.multiple_of(row * rows, rows), rows), :]


def gather_kernel(n_row, n_col, used, with_orbitals, *refs):
    refs = list(refs)
    ring_in, row_in = refs[:2]
    del refs[:2]
    orbitals = refs.pop(0) if with_orbitals else None
    panel, stack = refs[:2]
    del refs[:2]
    partner = refs.pop(0) if with_orbitals else None
    ring_hold, row_hold = refs[:2]
    del refs[:2]
    orbital_hold = refs.pop(0) if with_orbitals else None
    hold_in, hold_out, ring_send, ring_recv, row_send, row_recv = refs[:6]
    orbital_send, orbital_recv = refs[6:] if with_orbitals else (None, None)

    row, col = lax.axis_index("row"), lax.axis_index("col")
    place = ring_place(col, n_col)
    chips = n_row // 2
    chip, core = row // 2, row % 2
    pair = row + 1 - 2 * core
    rows = row_in.shape[1]

    barrier = pltpu.get_barrier_semaphore()
    for sign in (1, -1):
        pl.semaphore_signal(
            barrier,
            inc=1,
            device_id={"col": ring_col((place + sign + n_col) % n_col, n_col)},
            device_id_type=pl.DeviceIdType.MESH,
        )
    for d in range(1, n_row):
        pl.semaphore_signal(
            barrier,
            inc=1,
            device_id={"row": (row + d) % n_row},
            device_id_type=pl.DeviceIdType.MESH,
        )
    pl.semaphore_wait(barrier, n_row + 1)

    def ring(step, way):
        return ring_copy(ring_in, panel, used, place, n_col, step, way, ring_send, ring_recv)

    def across(d):
        target = pair if d == 0 else (chip + d) % chips * 2 + core
        return remote(
            row_in, row_part(stack, row, rows), row_send.at[d], row_recv.at[d], row=target
        )

    def onward(d):
        held = row_part(stack, (chip - d + chips) % chips * 2 + core, rows)
        k = chips - 1 + d
        return remote(held, held, row_send.at[k], row_recv.at[k], row=pair)

    ring(0, 0).start()
    ring(0, 1).start()
    for d in range(1, chips):
        across(d).start()
    across(0).start()

    if with_orbitals:
        blocks = partner.shape[0]
        part = blocks // 2
        ratio = n_col // n_row
        source = col // ratio
        own = orbitals.at[pl.ds(col % ratio * blocks, blocks)]
        here = chip == source // 2
        is_source = row == source

        def to_pair():
            return remote(own, partner, orbital_send.at[0], orbital_recv.at[0], row=pair)

        def to_chip(d, h):
            k = 1 + 2 * (d - 1) + h
            return remote(
                orbitals.at[pl.ds(col % ratio * blocks + h * part, part)],
                partner.at[pl.ds(h * part, part)],
                orbital_send.at[k],
                orbital_recv.at[1],
                row=(chip + d) % chips * 2 + h,
            )

        def half_onward():
            held = partner.at[pl.ds(core * part, part)]
            return remote(
                held, held, orbital_send.at[2 * chips - 1], orbital_recv.at[2], row=pair
            )

        @pl.when(is_source)
        def _():
            for d in range(1, chips):
                for h in range(2):
                    to_chip(d, h).start()
            to_pair().start()

    ins = [(ring_in.at[:, pl.ds(0, used), :], ring_hold), (row_in, row_hold)]
    outs = [
        (ring_hold, panel.at[col, :, pl.ds(0, used), :]),
        (row_hold, row_part(stack, row, rows)),
    ]
    for k in range(2):
        pltpu.make_async_copy(*ins[k], hold_in.at[k]).start()
    for k in range(2):
        pltpu.make_async_copy(*ins[k], hold_in.at[k]).wait()
        pltpu.make_async_copy(*outs[k], hold_out.at[k]).start()
    if with_orbitals:

        @pl.when(is_source)
        def _():
            fetch = pltpu.make_async_copy(own, orbital_hold, hold_in.at[2])
            fetch.start()
            fetch.wait()
            pltpu.make_async_copy(orbital_hold, partner, hold_out.at[2]).start()

    for step in range(n_col - 1):
        for way in range(2):
            ring(step, way).wait_recv()
            if step < n_col - 2:
                ring(step + 1, way).start()
        if step == min(2, n_col - 2):
            for d in range(1, chips):
                across(d).wait_recv()
                onward(d).start()
        if with_orbitals and step == n_col - 3:

            @pl.when(jnp.logical_not(here))
            def _():
                to_chip(1, 0).wait_recv()
                half_onward().start()

    across(0).wait_recv()
    for d in range(1, chips):
        onward(d).wait_recv()
        onward(d).wait_send()
        across(d).wait_send()
    across(0).wait_send()
    if with_orbitals:

        @pl.when(is_source)
        def _():
            for d in range(1, chips):
                for h in range(2):
                    to_chip(d, h).wait_send()
            to_pair().wait_send()
            pltpu.make_async_copy(orbital_hold, partner, hold_out.at[2]).wait()

        @pl.when(here & jnp.logical_not(is_source))
        def _():
            to_pair().wait_recv()

        @pl.when(jnp.logical_not(here))
        def _():
            half_onward().wait_recv()
            half_onward().wait_send()

    for step in range(n_col - 1):
        for way in range(2):
            ring(step, way).wait_send()
    for k in range(2):
        pltpu.make_async_copy(*outs[k], hold_out.at[k]).wait()


def gather(fractions, largest, first_id, *arrays):
    slots = arrays[0].shape[1] // BS
    caps = sorted({-(-slots * part // 16) for part in fractions})
    branches = [
        functools.partial(gather_slots, cap * BS, first_id + k) for k, cap in enumerate(caps)
    ]
    index = sum((largest > cap).astype(jnp.int32) for cap in caps[:-1])
    return lax.switch(index, branches, *arrays)


def gather_slots(used, collective_id, ring_in, row_in, orbitals=None):
    n_row, n_col = lax.axis_size("row"), lax.axis_size("col")
    panel = jax.ShapeDtypeStruct((n_col,) + ring_in.shape, ring_in.dtype)
    stack = jax.ShapeDtypeStruct(
        (row_in.shape[0], n_row * row_in.shape[1], row_in.shape[2]), row_in.dtype
    )
    operands, results = [ring_in, row_in], [panel, stack]
    hold = (ring_in.shape[0], used, ring_in.shape[2])
    holds = [pltpu.VMEM(hold, ring_in.dtype), pltpu.VMEM(row_in.shape, row_in.dtype)]
    dma = pltpu.SemaphoreType.DMA
    sems = [dma((3,)), dma((3,)), dma((2, n_col - 1)), dma((2, n_col - 1))]
    sems += [dma((n_row - 1,)), dma((n_row - 1,))]
    if orbitals is not None:
        blocks = orbitals.shape[0] * n_row // n_col
        partner = (blocks,) + orbitals.shape[1:]
        operands.append(orbitals)
        results.append(jax.ShapeDtypeStruct(partner, orbitals.dtype))
        holds.append(pltpu.VMEM(partner, orbitals.dtype))
        sems += [dma((n_row,)), dma((3,))]
    return pl.pallas_call(
        functools.partial(gather_kernel, n_row, n_col, used, orbitals is not None),
        out_shape=results,
        in_specs=[pl.BlockSpec(memory_space=pl.ANY)] * len(operands),
        out_specs=[pl.BlockSpec(memory_space=pl.ANY)] * len(results),
        scratch_shapes=holds + sems,
        compiler_params=pltpu.CompilerParams(
            collective_id=collective_id, has_side_effects=True
        ),
    )(*operands)


def reduce_kernel(axis, size, in_ref, out_ref, landed, own_sem, send, recv):
    me = lax.axis_index(axis)
    barrier = pltpu.get_barrier_semaphore()
    for d in range(1, size):
        pl.semaphore_signal(
            barrier,
            inc=1,
            device_id={axis: (me + d) % size},
            device_id_type=pl.DeviceIdType.MESH,
        )
    own = pltpu.make_async_copy(in_ref.at[me], landed.at[0], own_sem)
    own.start()
    pl.semaphore_wait(barrier, size - 1)
    copies = []
    for d in range(1, size):
        target = (me + d) % size
        copies.append(
            remote(in_ref.at[target], landed.at[d], send.at[d], recv.at[d], **{axis: target})
        )
        copies[-1].start()
    own.wait()
    for copy in copies:
        copy.wait_recv()
    out_ref[...] = jnp.sum(landed[...], axis=0)
    for copy in copies:
        copy.wait_send()


def reduce_over(axis, terms, collective_id):
    size = terms.shape[0]
    dma = pltpu.SemaphoreType.DMA
    return pl.pallas_call(
        functools.partial(reduce_kernel, axis, size),
        out_shape=jax.ShapeDtypeStruct(terms.shape[1:], terms.dtype),
        in_specs=[pl.BlockSpec(memory_space=pl.ANY)],
        out_specs=pl.BlockSpec(memory_space=pltpu.VMEM),
        scratch_shapes=[pltpu.VMEM(terms.shape, terms.dtype), dma, dma((size,)), dma((size,))],
        compiler_params=pltpu.CompilerParams(
            collective_id=collective_id, has_side_effects=True
        ),
    )(terms)


def block_slots(block_mask, row_index, row_blocks, col_blocks):
    tiles = lax.dynamic_slice_in_dim(block_mask, row_index * row_blocks, row_blocks, 0)
    tiles = tiles.reshape(row_blocks, -1, col_blocks).transpose(1, 0, 2)
    tiles = tiles.reshape(tiles.shape[0], row_blocks * col_blocks)
    return jnp.where(tiles > 0, jnp.cumsum(tiles, axis=1) - 1, -1).astype(jnp.int32)


def largest_count(block_mask, row_blocks, col_blocks):
    rows, cols = block_mask.shape
    tiles = block_mask.reshape(rows // row_blocks, row_blocks, cols // col_blocks, col_blocks)
    return jnp.max(jnp.sum(tiles, axis=(1, 3)))


def pack_kernel(slots, values_ref, out_ref):
    col_blocks = values_ref.shape[2] // BS
    for k in range(out_ref.shape[1] // BS):
        a, b = divmod(k, col_blocks)

        @pl.when(slots[k] >= 0)
        def _():
            start = pl.multiple_of(slots[k] * BS, BS)
            out_ref[:, pl.ds(start, BS), :] = values_ref[
                :, a * BS : (a + 1) * BS, b * BS : (b + 1) * BS
            ]


def pack(values, slots):
    lead, rows, cols = values.shape
    return pl.pallas_call(
        pack_kernel,
        out_shape=jax.ShapeDtypeStruct((lead, rows * cols // BS, BS), values.dtype),
        in_specs=[
            pl.BlockSpec(memory_space=pltpu.SMEM),
            pl.BlockSpec(memory_space=pltpu.VMEM),
        ],
        out_specs=pl.BlockSpec(memory_space=pltpu.VMEM),
    )(slots, values)


def product_kernel(slots, keep, left_ref, right_ref, out_ref, dense, total):
    step = pl.program_id(0)
    rows, depth = dense.shape[1:]
    col_blocks = depth // BS
    count = rows // BS * col_blocks
    for k in range(count):
        a, b = divmod(k, col_blocks)
        slot = slots[step * count + k]

        @pl.when(slot >= 0)
        def _():
            start = pl.multiple_of(slot * BS, BS)
            dense[:, a * BS : (a + 1) * BS, b * BS : (b + 1) * BS] = left_ref[
                0, :, pl.ds(start, BS), :
            ]

        @pl.when(slot < 0)
        def _():
            dense[:, a * BS : (a + 1) * BS, b * BS : (b + 1) * BS] = jnp.zeros(
                (dense.shape[0], BS, BS), dense.dtype
            )

    for v in range(total.shape[0]):
        term = jnp.dot(
            dense[min(v, dense.shape[0] - 1)],
            right_ref[min(v, right_ref.shape[0] - 1)],
            preferred_element_type=jnp.float32,
        )

        @pl.when(step == 0)
        def _():
            total[v] = term

        @pl.when(step > 0)
        def _():
            total[v] += term

    @pl.when(step == pl.num_programs(0) - 1)
    def _():
        wide = out_ref.shape[2] // BS
        for a in range(rows // BS):
            for b in range(wide):
                block = total[:, a * BS : (a + 1) * BS, b * BS : (b + 1) * BS]
                block = block * keep[a * wide + b].astype(jnp.float32)
                out_ref[:, a * BS : (a + 1) * BS, b * BS : (b + 1) * BS] = block.astype(
                    out_ref.dtype
                )


def product(panel, slots, right, keep):
    steps, lead, packed, _ = panel.shape
    depth = right.shape[1] // steps
    rows = packed * BS // depth
    width = right.shape[2]
    vectors = max(lead, right.shape[0])
    return pl.pallas_call(
        product_kernel,
        out_shape=jax.ShapeDtypeStruct((vectors, rows, width), panel.dtype),
        grid_spec=pltpu.PrefetchScalarGridSpec(
            num_scalar_prefetch=2,
            grid=(steps,),
            in_specs=[
                pl.BlockSpec((1, lead, packed, BS), lambda c, a, b: (c, 0, 0, 0)),
                pl.BlockSpec((right.shape[0], depth, width), lambda c, a, b: (0, c, 0)),
            ],
            out_specs=pl.BlockSpec((vectors, rows, width), lambda c, a, b: (0, 0, 0)),
            scratch_shapes=[
                pltpu.VMEM((lead, rows, depth), panel.dtype),
                pltpu.VMEM((vectors, rows, width), jnp.float32),
            ],
        ),
        compiler_params=pltpu.CompilerParams(dimension_semantics=("arbitrary",)),
    )(slots.reshape(-1), keep.reshape(-1), panel, right)


def local(
    p_valence,
    p_conduction,
    trial_vectors,
    mask_valence,
    mask_conduction,
    mask_trial,
    orbitals,
    sphere_starts,
):
    row_index = lax.axis_index("row")
    col_index = lax.axis_index("col")
    vector_count, local_rows, local_cols = trial_vectors.shape
    row_blocks = local_rows // BS
    col_blocks = local_cols // BS
    conduction = masked(p_conduction, mask_conduction, row_index, col_index)
    trial_slots = block_slots(mask_trial, row_index, row_blocks, col_blocks)
    valence_slots = block_slots(mask_valence, row_index, row_blocks, col_blocks)
    trials = pack(trial_vectors, lax.dynamic_index_in_dim(trial_slots, col_index, 0, False))
    valence = pack(p_valence[None], lax.dynamic_index_in_dim(valence_slots, col_index, 0, False))
    trial_largest = largest_count(mask_trial, row_blocks, col_blocks)
    valence_largest = largest_count(mask_valence, row_blocks, col_blocks)
    keep = lax.dynamic_slice(
        mask_trial, (row_index * row_blocks, col_index * col_blocks), (row_blocks, col_blocks)
    )
    panels, conduction_cols, partner = gather(
        (8, 9, 10, 12, 16), trial_largest, 2, trials, conduction[None], orbitals
    )
    response = product(panels, trial_slots, conduction_cols, jnp.ones_like(keep))
    valence_rows, gathered = gather((11, 12, 13, 16), valence_largest, 7, valence, response)
    kernel = product(valence_rows, valence_slots, gathered, keep)
    starts_rows = lax.dynamic_slice_in_dim(sphere_starts, row_index * row_blocks, row_blocks, 0)
    starts_cols = lax.dynamic_slice_in_dim(sphere_starts, col_index * col_blocks, col_blocks, 0)
    slab_count = lax.axis_size("row") * lax.axis_size("col")
    density_grid = collocate(kernel, orbitals, partner, starts_rows, starts_cols, slab_count)
    n_row, n_col = lax.axis_size("row"), lax.axis_size("col")
    terms = density_grid.reshape(n_row, n_col, vector_count, SP)
    density = reduce_over("col", reduce_over("row", terms, 0), 1)
    return (kernel, density)


def solution(mesh):
    placed = (
        P("row", "col"),
        P("row", "col"),
        P(None, "row", "col"),
        P(),
        P(),
        P(),
        P("row", None, None),
        P(),
    )
    return jax.shard_map(
        local,
        mesh=mesh,
        in_specs=placed,
        out_specs=(P(None, "row", "col"), P(None, ("row", "col"))),
        check_vma=False,
    )
```

```python
import functools

import jax
import jax.numpy as jnp
from jax import lax
from jax.experimental import pallas as pl
from jax.experimental.pallas import tpu as pltpu
from jax.sharding import PartitionSpec as P

BS = 128
SPAN = 16
SP = 512


def masked(values, block_mask, row_index, col_index):
    leading_dims = values.shape[:-2]
    row_blocks = values.shape[-2] // BS
    col_blocks = values.shape[-1] // BS
    tile_mask = lax.dynamic_slice(
        block_mask, (row_index * row_blocks, col_index * col_blocks), (row_blocks, col_blocks)
    ).astype(values.dtype)
    shaped = values.reshape(leading_dims + (row_blocks, BS, col_blocks, BS))
    return (shaped * tile_mask[:, None, :, None]).reshape(values.shape)


def collocate_kernel(row_blocks, col_blocks, starts_rows, starts_cols, keep, kernel_ref, *refs):
    row_refs = refs[:row_blocks]
    col_refs = refs[row_blocks : row_blocks + col_blocks]
    out_ref, frame_ref = refs[row_blocks + col_blocks :]
    slab = pl.program_id(0)
    vectors = kernel_ref.shape[0]
    group = 2 if col_blocks % 2 == 0 else 1
    groups = col_blocks // group

    def inside(start):
        shift = slab - start
        return ((shift >= 0) & (shift < SPAN)).astype(jnp.int32)

    seen = [inside(starts_cols[j]) for j in range(col_blocks)]
    for j in range(col_blocks):

        @pl.when(seen[j] > 0)
        def _():
            frame_ref[j * BS : (j + 1) * BS, :] = col_refs[j][0]

        @pl.when(seen[j] == 0)
        def _():
            frame_ref[j * BS : (j + 1) * BS, :] = jnp.zeros((BS, SP), frame_ref.dtype)

    out_ref[...] = jnp.zeros_like(out_ref)
    for i in range(row_blocks):
        needed = []
        for g in range(groups):
            uses = sum(seen[j] * keep[i * col_blocks + j] for j in range(g * group, (g + 1) * group))
            needed.append((inside(starts_rows[i]) > 0) & (uses > 0))
        for lo in range(groups):
            for hi in range(lo + 1, groups + 1):
                chosen = needed[lo] & needed[hi - 1]
                for g in range(groups):
                    if g < lo or g >= hi:
                        chosen = chosen & jnp.logical_not(needed[g])

                @pl.when(chosen)
                def _():
                    own = row_refs[i][0].astype(jnp.float32)
                    deep = slice(lo * group * BS, hi * group * BS)
                    left = kernel_ref[:, i * BS : (i + 1) * BS, deep]
                    left = left.reshape(vectors * BS, (hi - lo) * group * BS)
                    applied = jnp.dot(
                        left, frame_ref[deep, :], preferred_element_type=jnp.float32
                    )
                    for v in range(vectors):
                        term = own * applied[v * BS : (v + 1) * BS]
                        out_ref[0, v : v + 1, :] += jnp.sum(term, axis=0, keepdims=True)


def orbital_spec(block, place, which):
    def index_map(slab, starts_rows, starts_cols, keep):
        start = (starts_rows, starts_cols)[which][block]
        return place, 0, jnp.clip(slab - start, 0, SPAN - 1)

    return pl.BlockSpec((1, BS, SP), index_map)


def collocate(kernel, keep, orbitals, partners, starts_rows, starts_cols, slab_count):
    vector_count = kernel.shape[0]
    row_blocks = orbitals.shape[0]
    places = [(part, k) for part in partners for k in range(part.shape[0])]
    col_blocks = len(places)
    return pl.pallas_call(
        functools.partial(collocate_kernel, row_blocks, col_blocks),
        out_shape=jax.ShapeDtypeStruct((slab_count, vector_count, SP), jnp.float32),
        grid_spec=pltpu.PrefetchScalarGridSpec(
            num_scalar_prefetch=3,
            grid=(slab_count,),
            in_specs=[pl.BlockSpec(kernel.shape, lambda slab, a, b, c: (0, 0, 0))]
            + [orbital_spec(i, i, 0) for i in range(row_blocks)]
            + [orbital_spec(j, places[j][1], 1) for j in range(col_blocks)],
            out_specs=pl.BlockSpec((1, vector_count, SP), lambda slab, a, b, c: (slab, 0, 0)),
            scratch_shapes=[pltpu.VMEM((col_blocks * BS, SP), jnp.bfloat16)],
        ),
        compiler_params=pltpu.CompilerParams(dimension_semantics=("arbitrary",)),
    )(
        starts_rows,
        starts_cols,
        keep.reshape(-1),
        kernel,
        *([orbitals] * row_blocks),
        *[part for part, _ in places],
    )


def ring_place(col, size):
    odd = col % 2
    return (col // 2) * (1 - odd) + (size - 1 - col // 2) * odd


def ring_col(place, size):
    far = place // (size // 2)
    return 2 * place * (1 - far) + (2 * (size - 1 - place) + 1) * far


def remote(src, dst, send_sem, recv_sem, **where):
    return pltpu.make_async_remote_copy(
        src_ref=src,
        dst_ref=dst,
        send_sem=send_sem,
        recv_sem=recv_sem,
        device_id=where,
        device_id_type=pl.DeviceIdType.MESH,
    )


def ring_copy(mine, panel, used, place, size, step, way, send, recv):
    rows = used // 2
    sign = 1 - 2 * way
    owner = ring_col((place - sign * step + size) % size, size)
    half = pl.ds(way * rows, rows)
    held = panel.at[owner, :, half, :]
    src = mine.at[:, half, :] if step == 0 else held
    target = ring_col((place + sign + size) % size, size)
    return remote(src, held, send.at[way, step], recv.at[way, step], col=target)


def row_part(stack, row, rows):
    return stack.at[:, pl.ds(pl.multiple_of(row * rows, rows), rows), :]


def gather_kernel(n_row, n_col, used, span, with_orbitals, *refs):
    refs = list(refs)
    ring_in, row_in = refs[:2]
    del refs[:2]
    orbitals = refs.pop(0) if with_orbitals else None
    panel, stack = refs[:2]
    del refs[:2]
    partner = refs.pop(0) if with_orbitals else None
    ring_hold, row_hold = refs[:2]
    del refs[:2]
    orbital_hold = refs.pop(0) if with_orbitals else None
    hold_in, hold_out, ring_send, ring_recv, row_send, row_recv = refs[:6]
    orbital_send, orbital_recv = refs[6:] if with_orbitals else (None, None)

    row, col = lax.axis_index("row"), lax.axis_index("col")
    place = ring_place(col, n_col)
    chips = n_row // 2
    chip, core = row // 2, row % 2
    pair = row + 1 - 2 * core
    rows = row_in.shape[1]

    barrier = pltpu.get_barrier_semaphore()
    for sign in (1, -1):
        pl.semaphore_signal(
            barrier,
            inc=1,
            device_id={"col": ring_col((place + sign + n_col) % n_col, n_col)},
            device_id_type=pl.DeviceIdType.MESH,
        )
    for d in range(1, n_row):
        pl.semaphore_signal(
            barrier,
            inc=1,
            device_id={"row": (row + d) % n_row},
            device_id_type=pl.DeviceIdType.MESH,
        )
    pl.semaphore_wait(barrier, n_row + 1)

    def ring(step, way):
        return ring_copy(ring_in, panel, used, place, n_col, step, way, ring_send, ring_recv)

    def across(d):
        target = pair if d == 0 else (chip + d) % chips * 2 + core
        return remote(
            row_in, row_part(stack, row, rows), row_send.at[d], row_recv.at[d], row=target
        )

    def onward(d):
        held = row_part(stack, (chip - d + chips) % chips * 2 + core, rows)
        k = chips - 1 + d
        return remote(held, held, row_send.at[k], row_recv.at[k], row=pair)

    ring(0, 0).start()
    ring(0, 1).start()
    for d in range(1, chips):
        across(d).start()
    across(0).start()

    if with_orbitals:
        offset, count, blocks = span
        part = partner.shape[1] // 2
        ratio = n_col // n_row
        source = col // ratio
        first = col % ratio * blocks + offset
        own = orbitals.at[pl.ds(first, count)]
        here = chip == source // 2
        is_source = row == source

        def to_pair():
            return remote(own, partner, orbital_send.at[0], orbital_recv.at[0], row=pair)

        def to_chip(d, h, k):
            return remote(
                orbitals.at[pl.ds(first + k, 1), pl.ds(h * part, part)],
                partner.at[pl.ds(k, 1), pl.ds(h * part, part)],
                orbital_send.at[1 + (2 * (d - 1) + h) * count + k],
                orbital_recv.at[1 + k],
                row=(chip + d) % chips * 2 + h,
            )

        def half_onward(k):
            held = partner.at[pl.ds(k, 1), pl.ds(pl.multiple_of(core * part, part), part)]
            return remote(
                held,
                held,
                orbital_send.at[1 + 2 * (chips - 1) * count + k],
                orbital_recv.at[1 + count + k],
                row=pair,
            )

        @pl.when(is_source)
        def _():
            for k in range(count):
                for d in range(1, chips):
                    for h in range(2):
                        to_chip(d, h, k).start()
            to_pair().start()

    ins = [(ring_in.at[:, pl.ds(0, used), :], ring_hold), (row_in, row_hold)]
    outs = [
        (ring_hold, panel.at[col, :, pl.ds(0, used), :]),
        (row_hold, row_part(stack, row, rows)),
    ]
    for k in range(2):
        pltpu.make_async_copy(*ins[k], hold_in.at[k]).start()
    for k in range(2):
        pltpu.make_async_copy(*ins[k], hold_in.at[k]).wait()
        pltpu.make_async_copy(*outs[k], hold_out.at[k]).start()
    if with_orbitals:

        @pl.when(is_source)
        def _():
            fetch = pltpu.make_async_copy(own, orbital_hold, hold_in.at[2])
            fetch.start()
            fetch.wait()
            pltpu.make_async_copy(orbital_hold, partner, hold_out.at[2]).start()

    for step in range(n_col - 1):
        for way in range(2):
            ring(step, way).wait_recv()
            if step < n_col - 2:
                ring(step + 1, way).start()
        if step == n_col - 3:
            for d in range(1, chips):
                across(d).wait_recv()
                onward(d).start()

    if with_orbitals:

        @pl.when(jnp.logical_not(here))
        def _():
            for k in range(count):
                to_chip(1, 0, k).wait_recv()
                half_onward(k).start()

    across(0).wait_recv()
    for d in range(1, chips):
        onward(d).wait_recv()
        onward(d).wait_send()
        across(d).wait_send()
    across(0).wait_send()
    if with_orbitals:

        @pl.when(is_source)
        def _():
            for d in range(1, chips):
                for h in range(2):
                    for k in range(count):
                        to_chip(d, h, k).wait_send()
            to_pair().wait_send()
            pltpu.make_async_copy(orbital_hold, partner, hold_out.at[2]).wait()

        @pl.when(here & jnp.logical_not(is_source))
        def _():
            to_pair().wait_recv()

        @pl.when(jnp.logical_not(here))
        def _():
            for k in range(count):
                half_onward(k).wait_recv()
                half_onward(k).wait_send()

    for step in range(n_col - 1):
        for way in range(2):
            ring(step, way).wait_send()
    for k in range(2):
        pltpu.make_async_copy(*outs[k], hold_out.at[k]).wait()


def gather(fractions, largest, first_id, span, *arrays):
    slots = arrays[0].shape[1] // BS
    caps = sorted({-(-slots * part // 16) for part in fractions})
    branches = [
        functools.partial(gather_slots, cap * BS, first_id + k, span) for k, cap in enumerate(caps)
    ]
    index = sum((largest > cap).astype(jnp.int32) for cap in caps[:-1])
    return lax.switch(index, branches, *arrays)


def gather_slots(used, collective_id, span, ring_in, row_in, orbitals=None):
    n_row, n_col = lax.axis_size("row"), lax.axis_size("col")
    panel = jax.ShapeDtypeStruct((n_col,) + ring_in.shape, ring_in.dtype)
    stack = jax.ShapeDtypeStruct(
        (row_in.shape[0], n_row * row_in.shape[1], row_in.shape[2]), row_in.dtype
    )
    operands, results = [ring_in, row_in], [panel, stack]
    hold = (ring_in.shape[0], used, ring_in.shape[2])
    holds = [pltpu.VMEM(hold, ring_in.dtype), pltpu.VMEM(row_in.shape, row_in.dtype)]
    dma = pltpu.SemaphoreType.DMA
    sems = [dma((3,)), dma((3,)), dma((2, n_col - 1)), dma((2, n_col - 1))]
    sems += [dma((n_row - 1,)), dma((n_row - 1,))]
    if orbitals is not None:
        count, chips = span[1], n_row // 2
        partner = (count,) + orbitals.shape[1:]
        operands.append(orbitals)
        results.append(jax.ShapeDtypeStruct(partner, orbitals.dtype))
        holds.append(pltpu.VMEM(partner, orbitals.dtype))
        sems += [dma((1 + (2 * chips - 1) * count,)), dma((1 + 2 * count,))]
    return pl.pallas_call(
        functools.partial(gather_kernel, n_row, n_col, used, span, orbitals is not None),
        out_shape=results,
        in_specs=[pl.BlockSpec(memory_space=pl.ANY)] * len(operands),
        out_specs=[pl.BlockSpec(memory_space=pl.ANY)] * len(results),
        scratch_shapes=holds + sems,
        compiler_params=pltpu.CompilerParams(
            collective_id=collective_id, has_side_effects=True
        ),
    )(*operands)


def reduce_kernel(axis, size, in_ref, out_ref, landed, own_sem, send, recv):
    me = lax.axis_index(axis)
    barrier = pltpu.get_barrier_semaphore()
    for d in range(1, size):
        pl.semaphore_signal(
            barrier,
            inc=1,
            device_id={axis: (me + d) % size},
            device_id_type=pl.DeviceIdType.MESH,
        )
    own = pltpu.make_async_copy(in_ref.at[me], landed.at[0], own_sem)
    own.start()
    pl.semaphore_wait(barrier, size - 1)
    copies = []
    for d in range(1, size):
        target = (me + d) % size
        copies.append(
            remote(in_ref.at[target], landed.at[d], send.at[d], recv.at[d], **{axis: target})
        )
        copies[-1].start()
    own.wait()
    for copy in copies:
        copy.wait_recv()
    out_ref[...] = jnp.sum(landed[...], axis=0)
    for copy in copies:
        copy.wait_send()


def reduce_over(axis, terms, collective_id):
    size = terms.shape[0]
    dma = pltpu.SemaphoreType.DMA
    return pl.pallas_call(
        functools.partial(reduce_kernel, axis, size),
        out_shape=jax.ShapeDtypeStruct(terms.shape[1:], terms.dtype),
        in_specs=[pl.BlockSpec(memory_space=pl.ANY)],
        out_specs=pl.BlockSpec(memory_space=pltpu.VMEM),
        scratch_shapes=[pltpu.VMEM(terms.shape, terms.dtype), dma, dma((size,)), dma((size,))],
        compiler_params=pltpu.CompilerParams(
            collective_id=collective_id, has_side_effects=True
        ),
    )(terms)


def block_slots(block_mask, row_index, row_blocks, col_blocks):
    tiles = lax.dynamic_slice_in_dim(block_mask, row_index * row_blocks, row_blocks, 0)
    tiles = tiles.reshape(row_blocks, -1, col_blocks).transpose(1, 0, 2)
    tiles = tiles.reshape(tiles.shape[0], row_blocks * col_blocks)
    return jnp.where(tiles > 0, jnp.cumsum(tiles, axis=1) - 1, -1).astype(jnp.int32)


def largest_count(block_mask, row_blocks, col_blocks):
    rows, cols = block_mask.shape
    tiles = block_mask.reshape(rows // row_blocks, row_blocks, cols // col_blocks, col_blocks)
    return jnp.max(jnp.sum(tiles, axis=(1, 3)))


def pack_kernel(slots, values_ref, out_ref):
    col_blocks = values_ref.shape[2] // BS
    for k in range(out_ref.shape[1] // BS):
        a, b = divmod(k, col_blocks)

        @pl.when(slots[k] >= 0)
        def _():
            start = pl.multiple_of(slots[k] * BS, BS)
            out_ref[:, pl.ds(start, BS), :] = values_ref[
                :, a * BS : (a + 1) * BS, b * BS : (b + 1) * BS
            ]


def pack(values, slots):
    lead, rows, cols = values.shape
    return pl.pallas_call(
        pack_kernel,
        out_shape=jax.ShapeDtypeStruct((lead, rows * cols // BS, BS), values.dtype),
        in_specs=[
            pl.BlockSpec(memory_space=pltpu.SMEM),
            pl.BlockSpec(memory_space=pltpu.VMEM),
        ],
        out_specs=pl.BlockSpec(memory_space=pltpu.VMEM),
    )(slots, values)


def product_kernel(slots, keep, left_ref, right_ref, out_ref, dense, total):
    step = pl.program_id(0)
    rows, depth = dense.shape[1:]
    col_blocks = depth // BS
    count = rows // BS * col_blocks
    for k in range(count):
        a, b = divmod(k, col_blocks)
        slot = slots[step * count + k]

        @pl.when(slot >= 0)
        def _():
            start = pl.multiple_of(slot * BS, BS)
            dense[:, a * BS : (a + 1) * BS, b * BS : (b + 1) * BS] = left_ref[
                0, :, pl.ds(start, BS), :
            ]

        @pl.when(slot < 0)
        def _():
            dense[:, a * BS : (a + 1) * BS, b * BS : (b + 1) * BS] = jnp.zeros(
                (dense.shape[0], BS, BS), dense.dtype
            )

    for v in range(total.shape[0]):
        term = jnp.dot(
            dense[min(v, dense.shape[0] - 1)],
            right_ref[min(v, right_ref.shape[0] - 1)],
            preferred_element_type=jnp.float32,
        )

        @pl.when(step == 0)
        def _():
            total[v] = term

        @pl.when(step > 0)
        def _():
            total[v] += term

    @pl.when(step == pl.num_programs(0) - 1)
    def _():
        wide = out_ref.shape[2] // BS
        for a in range(rows // BS):
            for b in range(wide):
                block = total[:, a * BS : (a + 1) * BS, b * BS : (b + 1) * BS]
                block = block * keep[a * wide + b].astype(jnp.float32)
                out_ref[:, a * BS : (a + 1) * BS, b * BS : (b + 1) * BS] = block.astype(
                    out_ref.dtype
                )


def product(panel, slots, right, keep):
    steps, lead, packed, _ = panel.shape
    depth = right.shape[1] // steps
    rows = packed * BS // depth
    width = right.shape[2]
    vectors = max(lead, right.shape[0])
    return pl.pallas_call(
        product_kernel,
        out_shape=jax.ShapeDtypeStruct((vectors, rows, width), panel.dtype),
        grid_spec=pltpu.PrefetchScalarGridSpec(
            num_scalar_prefetch=2,
            grid=(steps,),
            in_specs=[
                pl.BlockSpec((1, lead, packed, BS), lambda c, a, b: (c, 0, 0, 0)),
                pl.BlockSpec((right.shape[0], depth, width), lambda c, a, b: (0, c, 0)),
            ],
            out_specs=pl.BlockSpec((vectors, rows, width), lambda c, a, b: (0, 0, 0)),
            scratch_shapes=[
                pltpu.VMEM((lead, rows, depth), panel.dtype),
                pltpu.VMEM((vectors, rows, width), jnp.float32),
            ],
        ),
        compiler_params=pltpu.CompilerParams(dimension_semantics=("arbitrary",)),
    )(slots.reshape(-1), keep.reshape(-1), panel, right)


def local(
    p_valence,
    p_conduction,
    trial_vectors,
    mask_valence,
    mask_conduction,
    mask_trial,
    orbitals,
    sphere_starts,
):
    row_index = lax.axis_index("row")
    col_index = lax.axis_index("col")
    vector_count, local_rows, local_cols = trial_vectors.shape
    row_blocks = local_rows // BS
    col_blocks = local_cols // BS
    conduction = masked(p_conduction, mask_conduction, row_index, col_index)
    trial_slots = block_slots(mask_trial, row_index, row_blocks, col_blocks)
    valence_slots = block_slots(mask_valence, row_index, row_blocks, col_blocks)
    trials = pack(trial_vectors, lax.dynamic_index_in_dim(trial_slots, col_index, 0, False))
    valence = pack(p_valence[None], lax.dynamic_index_in_dim(valence_slots, col_index, 0, False))
    trial_largest = largest_count(mask_trial, row_blocks, col_blocks)
    valence_largest = largest_count(mask_valence, row_blocks, col_blocks)
    keep = lax.dynamic_slice(
        mask_trial, (row_index * row_blocks, col_index * col_blocks), (row_blocks, col_blocks)
    )
    early = max(1, col_blocks * 3 // 4)
    panels, conduction_cols, partner_early = gather(
        (8, 9, 10, 12, 16),
        trial_largest,
        2,
        (0, early, col_blocks),
        trials,
        conduction[None],
        orbitals,
    )
    response = product(panels, trial_slots, conduction_cols, jnp.ones_like(keep))
    valence_rows, gathered, partner_late = gather(
        (11, 12, 13, 16),
        valence_largest,
        7,
        (early, col_blocks - early, col_blocks),
        valence,
        response,
        orbitals,
    )
    kernel = product(valence_rows, valence_slots, gathered, keep)
    starts_rows = lax.dynamic_slice_in_dim(sphere_starts, row_index * row_blocks, row_blocks, 0)
    starts_cols = lax.dynamic_slice_in_dim(sphere_starts, col_index * col_blocks, col_blocks, 0)
    slab_count = lax.axis_size("row") * lax.axis_size("col")
    density_grid = collocate(
        kernel, keep, orbitals, (partner_early, partner_late), starts_rows, starts_cols, slab_count
    )
    n_row, n_col = lax.axis_size("row"), lax.axis_size("col")
    terms = density_grid.reshape(n_row, n_col, vector_count, SP)
    density = reduce_over("col", reduce_over("row", terms, 0), 1)
    return (kernel, density)


def solution(mesh):
    placed = (
        P("row", "col"),
        P("row", "col"),
        P(None, "row", "col"),
        P(),
        P(),
        P(),
        P("row", None, None),
        P(),
    )
    return jax.shard_map(
        local,
        mesh=mesh,
        in_specs=placed,
        out_specs=(P(None, "row", "col"), P(None, ("row", "col"))),
        check_vma=False,
    )
```
